256 devices in a mesh: front: 8 (over z), lat: 32 (over y, x, core).
Axes of the slice: x: 4, y: 4, z: 8, core: 2. Of those that a mesh axis runs over, the one named last changes fastest.
Arguments:
- samples: float32 [128, 512, 128], P('front', 'lat'), may hold values from -6 to 6
- reaction: float32 [128, 512], P('front', 'lat'), may hold values from 0.5 to 2
- weight_x: float32 [128, 512], P('front', 'lat'), may hold values from 0.2 to 1
- weight_y: float32 [128, 512], P('front', 'lat'), may hold values from 0.2 to 1
- inverses: float32 [8, 64, 128, 128], P('front', 'lat'), may hold values from -0.3 to 0.4
- couplings: float32 [8, 64, 128, 128], P('front', 'lat'), may hold values from -12 to 12
Outputs:
- whitened: float32 [128, 512, 128], P('front', 'lat')
- gradients: float32 [3, 128, 512], P(None, 'front', 'lat')
The draws below stay inside these ranges and needn't reach their ends.
All inputs are finite; a program needn't handle non-finite values.
Results may differ from the reference program's by a relative error of at most 0.0003.
Values sent between devices are 32-bit elements; how exact they have to be, the bound alone decides.
No kernel may reach another device: no remote copies, remote signals or barrier semaphores. Data moves between devices by JAX's collectives and lax.ppermute only.
A program may use at most 192 MiB of HBM per device.

```python
import math
import jax
import jax.numpy as jnp
from jax import lax

W = 128
P_SIZE = 2
TX = 16
R = 128
TY = 16
GX = 128
GY = 512
BLOCKS = 512
N_FRONT = 8
N_LAT = 32


def factor_blocks(key):
    grand_accumulation = N_FRONT * N_LAT * P_SIZE
    half = W // 2
    scales = jax.random.uniform(jax.random.fold_in(key, 11), (grand_accumulation, W), jnp.float32, 0.15, 0.4)
    lower = jnp.clip(jax.random.normal(jax.random.fold_in(key, 12), (grand_accumulation, half, half), jnp.float32) * 0.125, -0.6, 0.6)
    exclusive_bound = jnp.zeros((grand_accumulation, W, W), jnp.float32).at[:, half:, :half].set(lower)
    rate = jnp.exp(jax.random.uniform(jax.random.fold_in(key, 13), (W,), jnp.float32, math.log(1.0 / grand_accumulation), math.log(1.0 / 30.0)))
    factor = jax.random.uniform(jax.random.fold_in(key, 14), (grand_accumulation,), jnp.float32, 0.6, 1.5)
    keep_indicator = 1.0 - rate[None, :] * factor[:, None]
    batch_shift = jax.random.randint(jax.random.fold_in(key, 15), (3,), 0, grand_accumulation)
    batch_cluster = jnp.any(jnp.arange(grand_accumulation)[:, None] == batch_shift[None, :], axis=1)
    keep_indicator = keep_indicator * jnp.where(batch_cluster, 0.8, 1.0)[:, None]
    eye = jnp.eye(W, dtype=jnp.float32)
    noise = jax.random.normal(jax.random.fold_in(key, 16), (grand_accumulation, W, W), jnp.float32) * 0.003
    mixing = noise + eye[None, :, :] * keep_indicator[:, :, None]
    inverse = (eye[None, :, :] + exclusive_bound) * scales[:, None, :]
    product = mixing - jnp.einsum('kij,kjl->kil', exclusive_bound, mixing, precision=lax.Precision.HIGHEST)
    coupling = -(1.0 / scales)[:, :, None] * product
    return (inverse.reshape(N_FRONT, N_LAT * P_SIZE, W, W), coupling.reshape(N_FRONT, N_LAT * P_SIZE, W, W))


def draw_inverses(key, part):
    return factor_blocks(key)[0]


def draw_couplings(key, part):
    return factor_blocks(key)[1]


def level_of(rng, extent, split, low, top_value):
    loudness = 1.0
    for axis_at, blocks in split:
        heights = jax.random.uniform(jax.random.fold_in(jax.random.fold_in(rng, 6), axis_at), (blocks,), jnp.float32, low / len(split), top_value / len(split))
        loudness = loudness * jnp.repeat(jnp.exp(heights), extent[axis_at] // blocks).reshape((-1,) + (1,) * (len(extent) - 1 - axis_at))
    return loudness


def centred(own_key, extent, deviation, limit, cuts=(), kind=jnp.bfloat16):
    values = deviation * jax.random.normal(own_key, extent, jnp.float32)
    if cuts:
        values = values * level_of(own_key, extent, cuts, -0.22, 0.18)
    return jnp.clip(values, -limit, limit).astype(kind)


def setup_inputs(seed: int = 0) -> dict:
    key_of = jax.random.split(jax.random.key(seed), 7)
    samples = centred(key_of[0], (GX, GY, R), 1.0, 6.0, ((0, 8), (1, 32)), jnp.float32)
    reaction = jnp.clip(jnp.exp(math.log(2.0) - 1.3862944 * jax.random.uniform(key_of[1], (GX, GY), jnp.float32) ** level_of(key_of[1], (GX, GY), ((0, 8), (1, 32)), -0.2, 0.2)), 0.5, 2.0)
    weight_x = jnp.clip(jnp.exp(math.log(1.0) - 1.609438 * jax.random.uniform(key_of[2], (GX, GY), jnp.float32) ** level_of(key_of[2], (GX, GY), ((0, 8), (1, 32)), -0.2, 0.2)), 0.2, 1.0)
    weight_y = jnp.clip(jnp.exp(math.log(1.0) - 1.609438 * jax.random.uniform(key_of[3], (GX, GY), jnp.float32) ** level_of(key_of[3], (GX, GY), ((0, 8), (1, 32)), -0.2, 0.2)), 0.2, 1.0)
    inverses = draw_inverses(jax.random.fold_in(key_of[6], 71), 0)
    couplings = draw_couplings(jax.random.fold_in(key_of[6], 71), 0)
    return dict(samples=samples, reaction=reaction, weight_x=weight_x, weight_y=weight_y, inverses=inverses, couplings=couplings)


def matmul(left, right):
    return jnp.dot(left, right, precision=lax.Precision.HIGHEST, preferred_element_type=jnp.float32)


def to_blocks(field):
    return field.reshape(N_FRONT, TX, N_LAT, TY, R).transpose(0, 2, 1, 3, 4).reshape(BLOCKS, W, R)


def from_blocks(blocks):
    return blocks.reshape(N_FRONT, N_LAT, TX, TY, R).transpose(0, 2, 1, 3, 4).reshape(GX, GY, R)


def reference(samples, reaction, weight_x, weight_y, inverses, couplings):
    padded = jnp.pad(samples, ((1, 1), (1, 1), (0, 0)))
    lap_x = 2.0 * samples - padded[:-2, 1:-1] - padded[2:, 1:-1]
    lap_y = 2.0 * samples - padded[1:-1, :-2] - padded[1:-1, 2:]
    resid = reaction[:, :, None] * samples + weight_x[:, :, None] * lap_x + weight_y[:, :, None] * lap_y
    blocks = to_blocks(resid)
    reciprocal_pieces = inverses.reshape(BLOCKS, W, W)
    lower_band_coupling = couplings.reshape(BLOCKS, W, W)

    def forward(running_carry, element_list):
        inverse_k, coupling_k, rhs_k = element_list
        result = matmul(inverse_k, rhs_k - matmul(coupling_k, running_carry))
        return result, result

    initial_carry = jnp.zeros((W, R), jnp.float32)
    unused_value, unknown_answer = lax.scan(forward, initial_carry, (reciprocal_pieces, lower_band_coupling, blocks))

    def upward_substitution(running_carry, element_list):
        inverse_k, coupling_k, solved_k = element_list
        result = matmul(inverse_k.T, solved_k - running_carry)
        return matmul(coupling_k.T, result), result

    unused_value, reverse_mode_pieces = lax.scan(upward_substitution, initial_carry, (reciprocal_pieces, lower_band_coupling, unknown_answer), reverse=True)
    whitened = from_blocks(reverse_mode_pieces)
    gradients = jnp.stack([jnp.mean(whitened * samples, axis=2), jnp.mean(whitened * lap_x, axis=2), jnp.mean(whitened * lap_y, axis=2)])
    return whitened, gradients
```

```python
import jax
import jax.numpy as jnp
from jax import lax
from jax.experimental import pallas as pl
from jax.experimental.pallas import tpu as pltpu
from jax.sharding import PartitionSpec as P

F32 = jnp.float32
BF16 = jnp.bfloat16
W = 128


def exchange(array, axis, mask):
    return lax.ppermute(array, axis, [(i, i ^ mask) for i in range(lax.axis_size(axis))])


def call(kernel, outs, *operands, flops=4e7):
    vmem = pl.BlockSpec(memory_space=pltpu.VMEM)
    traffic = sum(a.size * 4 for a in operands) + sum(a.size * 4 for a in outs)
    return pl.pallas_call(
        kernel,
        out_shape=outs,
        in_specs=[vmem] * len(operands),
        out_specs=[vmem] * len(outs),
        compiler_params=pltpu.CompilerParams(vmem_limit_bytes=16 << 20),
        cost_estimate=pl.CostEstimate(flops=int(flops), bytes_accessed=int(traffic), transcendentals=0),
    )(*operands)


def shaped(*dims):
    return jax.ShapeDtypeStruct(dims, F32)


def two(value):
    high = value.astype(BF16)
    return high, (value - high.astype(F32)).astype(BF16)


def three(value):
    high = value.astype(BF16)
    rest = value - high.astype(F32)
    middle = rest.astype(BF16)
    return high, middle, (rest - middle.astype(F32)).astype(BF16)


def product(left, right, contract=1):
    def one(a, b):
        return lax.dot_general(a, b, (((contract,), (0,)), ((), ())), preferred_element_type=F32)

    (ah, al), (bh, bl) = (two(left), two(right))
    return one(ah, bh) + (one(ah, bl) + one(al, bh))


def exact(left, right, contract=1):
    def one(a, b):
        return lax.dot_general(a, b, (((contract,), (0,)), ((), ())), preferred_element_type=F32)

    (ah, am, al), (bh, bm, bl) = (three(left), three(right))
    return one(ah, bh) + ((one(ah, bm) + one(am, bh)) + (one(am, bm) + (one(ah, bl) + one(al, bh))))


def compose(first, second):
    (xa, za), (xb, zb) = (first, second)
    upper = product(jnp.concatenate([xb[:, :W], zb[:, :W]], axis=0), xa)
    tail = jnp.concatenate([xb[:, W:], zb[:, W:]], axis=0)
    upper = jnp.concatenate([upper[:, :W], upper[:, W:] + tail], axis=1)
    return (upper[:W], za + product(xa[:, :W], upper[W:], 0))


def forward(first, xb):
    out = product(xb[:, :W], first)
    return jnp.concatenate([out[:, :W], out[:, W:] + xb[:, W:]], axis=1)


def choose(flag, one, other):
    return tuple(jnp.where(flag, a, b) for a, b in zip(one, other))


def ordered(late, partner, own):
    return (choose(late, partner, own), choose(late, own, partner))


def bit(axis, mask):
    return (lax.axis_index(axis) & mask) != 0


def edges(samples):
    def kernel(s, x_one, x_two, y_one, y_two):
        up = bit("front", 1)
        x_one[...] = jnp.where(up, s[0:1], s[15:16])
        x_two[...] = jnp.where(up, s[15:16], s[0:1])
        right = bit("lat", 1)
        y_one[...] = jnp.where(right, s[:, 0:1], s[:, 15:16])
        y_two[...] = jnp.where(right, s[:, 15:16], s[:, 0:1])

    x, y = (shaped(1, 16, W), shaped(16, 1, W))
    return call(kernel, [x, x, y, y], samples, flops=1)


def inside(axis, before, after):
    at, size = (lax.axis_index(axis), lax.axis_size(axis))
    return (jnp.where(at == 0, 0.0, before), jnp.where(at == size - 1, 0.0, after))


def matrices(inverses, couplings):
    def kernel(inv, cou, steps, total):
        f1 = -exact(inv[0, 0], cou[0, 0])
        f2 = -exact(inv[0, 1], cou[0, 1])
        steps[0] = f1
        steps[1] = f2
        both = exact(f2, f1)
        total[0] = both
        total[1] = exact(f1, f1 + exact(f2, both, 0), 0)

    return call(kernel, [shaped(2, W, W), shaped(2, W, W)], inverses, couplings, flops=3e7)


def sources(samples, halo, reaction, weight_x, weight_y, inverses, steps, total):
    def kernel(s, x1, x2, y1, y2, re, wx, wy, inv, st, to, lapx, lapy, local, element):
        v = s[...]
        xm, xp = choose(bit("front", 1), (x1[...], x2[...]), (x2[...], x1[...]))
        ym, yp = choose(bit("lat", 1), (y1[...], y2[...]), (y2[...], y1[...]))
        xm, xp = inside("front", xm, xp)
        ym, yp = inside("lat", ym, yp)
        lx = 2.0 * v - jnp.concatenate([xm, v[:-1]], axis=0) - jnp.concatenate([v[1:], xp], axis=0)
        ly = 2.0 * v - jnp.concatenate([ym, v[:, :-1]], axis=1) - jnp.concatenate([v[:, 1:], yp], axis=1)
        lapx[...] = lx
        lapy[...] = ly
        r = re[...][:, :, None] * v + wx[...][:, :, None] * lx + wy[...][:, :, None] * ly
        r = r.reshape(2, W, W)
        b1 = exact(inv[0, 0], r[0])
        b2 = exact(inv[0, 1], r[1])
        f1, f2 = (st[0], st[1])
        v2 = exact(f2, b1) + b2
        local[0] = b1
        local[1] = b2
        element[0] = jnp.concatenate([to[0], v2], axis=1)
        h1 = exact(f1, b1 + exact(f2, v2, 0), 0)
        element[1] = jnp.concatenate([to[1], h1], axis=1)

    tile, pair = (shaped(16, 16, W), shaped(2, W, W))
    outs = [tile, tile, pair, shaped(2, W, 2 * W)]
    return call(kernel, outs, samples, *halo, reaction, weight_x, weight_y, inverses, steps, total)


def pair_up(element, partner):
    def kernel(e, p, out, mine):
        late = bit("lat", 1)
        x, z = compose(*ordered(late, (p[0], p[1]), (e[0], e[1])))
        out[0] = x
        out[1] = z
        mine[...] = jnp.where(late, z, x)

    return call(kernel, [shaped(2, W, 2 * W), shaped(W, 2 * W)], element, partner)


def start_sides(partner):
    def kernel(p, before, after):
        late = bit("lat", 1)
        row = lax.broadcasted_iota(jnp.int32, (W, 2 * W), 0)
        col = lax.broadcasted_iota(jnp.int32, (W, 2 * W), 1)
        eye = jnp.where(row == col, 1.0, 0.0).astype(F32)
        before[...] = jnp.where(late, p[0], eye)
        after[0] = jnp.where(late, eye, p[0])
        after[1] = jnp.where(late, 0.0, p[1])

    return call(kernel, [shaped(W, 2 * W), shaped(2, W, 2 * W)], partner, flops=1)


def whole(got, other):
    return choose(bit("lat", 1), (other[...], got[...]), (got[...], other[...]))


def level(element, axis, mask, final):
    def kernel(e, g, o, earlier_sides, out, mine):
        late = bit(axis, mask)
        x, z = compose(*ordered(late, whole(g, o), (e[0], e[1])))
        out[0] = x
        out[1] = z
        odd = bit("lat", 1)
        if final:
            mine[...] = jnp.where(bit(*final), jnp.where(odd, z[:, W:], z[:, :W]), x[:, W:])
        else:
            mine[...] = jnp.where(odd, z, x)

    sent = shaped(W, W) if final else shaped(W, 2 * W)
    return lambda got, other, done: call(kernel, [shaped(2, W, 2 * W), sent], element, got, other, done)


def sides(before, after, got, other, axis, mask):
    def kernel(b, a, g, o, before_out, after_out):
        late = bit(axis, mask)
        px, pz = whole(g, o)

        @pl.when(late)
        def _():
            before_out[...] = forward(px, b[...])
            after_out[...] = a[...]

        @pl.when(jnp.logical_not(late))
        def _():
            before_out[...] = b[...]
            x, z = compose((a[0], a[1]), (px, pz))
            after_out[0] = x
            after_out[1] = z

    return call(kernel, [shaped(W, 2 * W), shaped(2, W, 2 * W)], before, after, got, other)


def respond(before, after, inverses, couplings, local, steps, axis, mask):
    def kernel(b, a, inv, cou, loc, st, out):
        late = bit(axis, mask)
        tail = jnp.concatenate
        none = jnp.zeros((W, W), F32)
        incoming = tail([jnp.where(late, b[:, :W], 0.0), b[:, W:]], axis=1)
        y1 = tail([none, loc[0]], axis=1) + exact(st[0], incoming)
        y2 = tail([none, loc[1]], axis=1) + exact(st[1], y1)
        back = tail([jnp.where(late, 0.0, a[0, :, :W].T), a[1, :, W:]], axis=1)
        x2 = exact(inv[0, 1], y2 + back + exact(a[1, :, :W], y2), 0)
        out[0] = exact(inv[0, 0], y1 - exact(cou[0, 1], x2, 0), 0)
        out[1] = x2

    return call(kernel, [shaped(2, W, 2 * W)], before, after, inverses, couplings, local, steps, flops=1e8)[0]


def finish(axis, mask, element, got, other, response, samples, lapx, lapy):
    def kernel(e, g, o, resp, s, lx, ly, white, grad):
        late = bit(axis, mask)
        odd = bit("lat", 1)
        matrix, vector = choose(odd, (o[...], g[...]), (g[...], o[...]))
        reach = vector + product(matrix, e[0, :, W:])
        comes = jnp.where(late, g[...], reach)
        r = resp[...].reshape(2 * W, 2 * W)
        w = (r[:, W:] + product(r[:, :W], comes)).reshape(16, 16, W)
        white[...] = w
        grad[0] = jnp.sum(w * s[...], axis=2) * (1.0 / W)
        grad[1] = jnp.sum(w * lx[...], axis=2) * (1.0 / W)
        grad[2] = jnp.sum(w * ly[...], axis=2) * (1.0 / W)

    outs = [shaped(16, 16, W), shaped(3, 16, 16)]
    return call(kernel, outs, element, got, other, response, samples, lapx, lapy)


LEVELS = (
    ("lat", 2, 2),
    ("lat", 4, 6),
    ("lat", 8, 8),
    ("lat", 16, 24),
    ("front", 1, 1),
    ("front", 2, 2),
)
TOP = ("front", 4, 6)


def body(samples, reaction, weight_x, weight_y, inverses, couplings):
    x_one, x_two, y_one, y_two = edges(samples)
    halo = []
    for axis, one, two_ in (("front", x_one, x_two), ("lat", y_one, y_two)):
        size = lax.axis_size(axis)
        odd = [(i, (i + 1) % size) for i in range(1, size, 2)]
        halo += [exchange(one, axis, 1), lax.ppermute(two_, axis, odd + [(j, i) for i, j in odd])]
    steps, total = matrices(inverses, couplings)
    lapx, lapy, local, element = sources(
        samples, halo, reaction, weight_x, weight_y, inverses, steps, total
    )
    partner = exchange(element, "lat", 1)
    element, mine = pair_up(element, partner)
    before, after = start_sides(partner)
    for at, (axis, mask, away) in enumerate(LEVELS):
        got = exchange(mine, axis, away)
        other = exchange(got, "lat", 1)
        final = TOP[:2] if at == len(LEVELS) - 1 else None
        element, mine = level(element, axis, mask, final)(got, other, before)
        before, after = sides(before, after, got, other, axis, mask)
    response = respond(before, after, inverses, couplings, local, steps, *TOP[:2])
    got = exchange(mine, TOP[0], TOP[2])
    other = exchange(got, "lat", 1)
    return tuple(finish(*TOP[:2], element, got, other, response, samples, lapx, lapy))


def solution(mesh):
    placed = (
        P("front", "lat", None),
        P("front", "lat"),
        P("front", "lat"),
        P("front", "lat"),
        P("front", "lat", None, None),
        P("front", "lat", None, None),
    )
    return jax.shard_map(
        body,
        mesh=mesh,
        in_specs=placed,
        out_specs=(P("front", "lat", None), P(None, "front", "lat")),
        check_vma=False,
    )
```

```python
import jax
import jax.numpy as jnp
from jax import lax
from jax.experimental import pallas as pl
from jax.experimental.pallas import tpu as pltpu
from jax.sharding import PartitionSpec as P

F32 = jnp.float32
BF16 = jnp.bfloat16
W = 128


EVERY = ("front", "lat")


def count():
    return lax.axis_size("front") * lax.axis_size("lat")


def send(array, pairs):
    return lax.ppermute(array, EVERY, pairs)


def swap(array):
    return send(array, [(i, i ^ 1) for i in range(count())])


def call(kernel, outs, *operands, flops=4e7, same=None):
    vmem = pl.BlockSpec(memory_space=pltpu.VMEM)
    traffic = sum(a.size * 4 for a in operands) + sum(a.size * 4 for a in outs)
    return pl.pallas_call(
        kernel,
        out_shape=outs,
        in_specs=[vmem] * len(operands),
        out_specs=[vmem] * len(outs),
        input_output_aliases=same or {},
        compiler_params=pltpu.CompilerParams(vmem_limit_bytes=16 << 20),
        cost_estimate=pl.CostEstimate(flops=int(flops), bytes_accessed=int(traffic), transcendentals=0),
    )(*operands)


def shaped(*dims):
    return jax.ShapeDtypeStruct(dims, F32)


def two(value):
    high = value.astype(BF16)
    return high, (value - high.astype(F32)).astype(BF16)


def three(value):
    high = value.astype(BF16)
    rest = value - high.astype(F32)
    middle = rest.astype(BF16)
    return high, middle, (rest - middle.astype(F32)).astype(BF16)


def product(left, right, contract=1):
    def one(a, b):
        return lax.dot_general(a, b, (((contract,), (0,)), ((), ())), preferred_element_type=F32)

    (ah, al), (bh, bl) = (two(left), two(right))
    return one(ah, bh) + (one(ah, bl) + one(al, bh))


def exact(left, right, contract=1):
    def one(a, b):
        return lax.dot_general(a, b, (((contract,), (0,)), ((), ())), preferred_element_type=F32)

    (ah, am, al), (bh, bm, bl) = (three(left), three(right))
    return one(ah, bh) + ((one(ah, bm) + one(am, bh)) + (one(am, bm) + (one(ah, bl) + one(al, bh))))


def compose(first, second):
    (xa, za), (xb, zb) = (first, second)
    upper = product(jnp.concatenate([xb[:, :W], zb[:, :W]], axis=0), xa)
    tail = jnp.concatenate([xb[:, W:], zb[:, W:]], axis=0)
    upper = jnp.concatenate([upper[:, :W], upper[:, W:] + tail], axis=1)
    return (upper[:W], za + product(xa[:, :W], upper[W:], 0))


def compose_vectors(fa, maps, a, b):
    out = product(maps, a[:W]) + b
    return out[:W], a[W:] + product(fa, out[W:], 0)


def compose_matrices(a, b):
    out = product(b, a[:W])
    return out[:W], a[W:] + product(a[:W], out[W:], 0)


def forward(first, xb):
    out = product(xb[:, :W], first)
    return jnp.concatenate([out[:, :W], out[:, W:] + xb[:, W:]], axis=1)


def choose(flag, one, other):
    return tuple(jnp.where(flag, a, b) for a, b in zip(one, other))


def place():
    return lax.axis_index("front") * lax.axis_size("lat") + lax.axis_index("lat")


def bit(mask):
    return (place() & mask) != 0


def edges(samples, inverses, couplings):
    def kernel(s, inv, cou, x_one, x_two, y_one, y_two, s_out, inv_out, cou_out, sems):
        pairs = ((s, s_out), (inv, inv_out), (cou, cou_out))
        copies = [pltpu.make_async_copy(a, b, sems.at[i]) for i, (a, b) in enumerate(pairs)]
        for copy in copies:
            copy.start()
        copies[0].wait()
        up = bit(UP)
        x_one[...] = jnp.where(up, s_out[0:1], s_out[15:16])
        x_two[...] = jnp.where(up, s_out[15:16], s_out[0:1])
        right = bit(1)
        y_one[...] = jnp.where(right, s_out[:, 0:1], s_out[:, 15:16])
        y_two[...] = jnp.where(right, s_out[:, 15:16], s_out[:, 0:1])
        copies[1].wait()
        copies[2].wait()

    x, y = (shaped(1, 16, W), shaped(16, 1, W))
    outs = [x, x, y, y] + [shaped(*a.shape) for a in (samples, inverses, couplings)]
    return pl.pallas_call(
        kernel,
        out_shape=outs,
        in_specs=[pl.BlockSpec(memory_space=pltpu.HBM)] * 3,
        out_specs=[pl.BlockSpec(memory_space=pltpu.VMEM)] * len(outs),
        scratch_shapes=[pltpu.SemaphoreType.DMA((3,))],
        compiler_params=pltpu.CompilerParams(vmem_limit_bytes=107 << 19),
        cost_estimate=pl.CostEstimate(flops=1, bytes_accessed=800000, transcendentals=0),
    )(samples, inverses, couplings)


def inside(axis, before, after):
    at, size = (lax.axis_index(axis), lax.axis_size(axis))
    return (jnp.where(at == 0, 0.0, before), jnp.where(at == size - 1, 0.0, after))


def matrices(inverses, couplings, *waits):
    def kernel(inv, cou, *refs):
        steps, total = refs[-2:]
        f1 = -exact(inv[0, 0], cou[0, 0])
        f2 = -exact(inv[0, 1], cou[0, 1])
        steps[0] = f1
        steps[1] = f2
        both = exact(f2, f1)
        total[:W] = both
        total[W:] = exact(f1, f1 + exact(f2, both, 0), 0)

    return call(kernel, [shaped(2, W, W), shaped(2 * W, W)], inverses, couplings, *waits, flops=3e7)


def sources(samples, halo, reaction, weight_x, weight_y, inverses, steps, *waits):
    def kernel(s, x1, x2, y1, y2, re, wx, wy, inv, st, *refs):
        lapx, lapy, local, vectors = refs[-4:]
        v = s[...]
        xm, xp = choose(bit(UP), (x1[...], x2[...]), (x2[...], x1[...]))
        ym, yp = choose(bit(1), (y1[...], y2[...]), (y2[...], y1[...]))
        xm, xp = inside("front", xm, xp)
        ym, yp = inside("lat", ym, yp)
        lx = 2.0 * v - jnp.concatenate([xm, v[:-1]], axis=0) - jnp.concatenate([v[1:], xp], axis=0)
        ly = 2.0 * v - jnp.concatenate([ym, v[:, :-1]], axis=1) - jnp.concatenate([v[:, 1:], yp], axis=1)
        lapx[...] = lx
        lapy[...] = ly
        r = re[...][:, :, None] * v + wx[...][:, :, None] * lx + wy[...][:, :, None] * ly
        r = r.reshape(2, W, W)
        b1 = exact(inv[0, 0], r[0])
        b2 = exact(inv[0, 1], r[1])
        f1, f2 = (st[0], st[1])
        v2 = exact(f2, b1) + b2
        local[0] = b1
        local[1] = b2
        vectors[:W] = v2
        vectors[W:] = exact(f1, b1 + exact(f2, v2, 0), 0)

    tile = shaped(16, 16, W)
    outs = [tile, tile, shaped(2, W, W), shaped(2 * W, W)]
    return call(kernel, outs, samples, *halo, reaction, weight_x, weight_y, inverses, steps, *waits)


def in_chip(total, partner, *waits):
    def kernel(t, p, *refs):
        chip = refs[-1]
        a, b = choose(bit(1), (p[...], t[...]), (t[...], p[...]))
        chip[:W], chip[W:] = compose_matrices(a, b)

    return call(kernel, [shaped(2 * W, W)], total, partner, *waits)[0]


def merge(got, bit_even, bit_odd, even, odd, own, theirs, got_odd=None, last=None, waits=()):
    def kernel(g, ev, od, ow, th, *refs):
        state, block = refs[-2:]

        @pl.when(bit(1))
        def _():
            late = bit(bit_odd)
            vectors = g if got_odd is None else refs[0]
            a, b = choose(late, (vectors[...], od[...]), (od[...], vectors[...]))
            maps_a, maps_b = choose(late, (th[...], ow[...]), (ow[...], th[...]))
            tail = jnp.concatenate
            first = (tail([maps_a[:W], a[:W]], axis=1), tail([maps_a[W:], a[W:]], axis=1))
            second = (tail([maps_b[:W], b[:W]], axis=1), tail([maps_b[W:], b[W:]], axis=1))
            x, z = compose(first, second)
            if last is None:
                block[:W] = x[:, :W]
                block[W:] = z[:, :W]
                state[:W] = x[:, W:]
                state[W:] = z[:, W:]
            else:
                block[: 2 * W] = g[...]
                block[2 * W :] = x[:, W:]
                state[...] = jnp.where(bit(last), z[:, W:], x[:, W:])

        @pl.when(jnp.logical_not(bit(1)))
        def _():
            if last is not None:
                state[...] = ev[W:]
            else:
                late = bit(bit_even)
                a, b = choose(late, (g[...], ev[...]), (ev[...], g[...]))
                state[:W], state[W:] = compose_matrices(a, b)

    outs = [shaped(2 * W, W)] * 3 if last is None else [shaped(2 * W, W), shaped(W, W), shaped(3 * W, W)]
    operands = (got, even, odd, own, theirs) + (() if got_odd is None else (got_odd,)) + tuple(waits)
    return call(kernel, outs, *operands, same={0: 0})


def arrived(array):
    def kernel(a, out):
        pass

    return call(kernel, [shaped(*array.shape)], array, flops=1e10, same={0: 0})[0]


def start_sides(matrices, vectors):
    def kernel(m, v, out):
        odd = bit(1)
        row = lax.broadcasted_iota(jnp.int32, (W, 2 * W), 0)
        col = lax.broadcasted_iota(jnp.int32, (W, 2 * W), 1)
        eye = jnp.where(row == col, 1.0, 0.0).astype(F32)
        x = jnp.concatenate([m[:W], v[:W]], axis=1)
        out[0] = jnp.where(odd, x, eye)
        out[1] = jnp.where(odd, eye, x)
        out[2] = jnp.where(odd, 0.0, jnp.concatenate([m[W:], v[W:]], axis=1))

    return call(kernel, [shaped(3, W, 2 * W)], matrices, vectors, flops=1)[0]


def widen(around, theirs, theirs_swapped, got, got_swapped, mask):
    def kernel(s, te, to, go, ge, out):
        odd = bit(1)
        late = bit(mask)
        m = jnp.where(odd, to[...], te[...])
        v = jnp.where(odd, go[...], ge[: 2 * W])

        @pl.when(late)
        def _():
            out[0] = forward(jnp.concatenate([m[:W], v[:W]], axis=1), s[0])
            out[1:] = s[1:]

        @pl.when(jnp.logical_not(late))
        def _():
            out[0] = s[0]
            later = (jnp.concatenate([m[:W], v[:W]], axis=1), jnp.concatenate([m[W:], v[W:]], axis=1))
            out[1], out[2] = compose((s[1], s[2]), later)

    operands = (around, theirs, theirs_swapped, got, got_swapped)
    return call(kernel, [shaped(3, W, 2 * W)], *operands)[0]


def respond(around, inverses, couplings, local, steps, mask):
    def kernel(ar, inv, cou, loc, st, out):
        late = bit(mask)
        tail = jnp.concatenate
        none = jnp.zeros((W, W), F32)
        incoming = tail([jnp.where(late, ar[0, :, :W], 0.0), ar[0, :, W:]], axis=1)
        y1 = tail([none, loc[0]], axis=1) + product(st[0], incoming)
        y2 = tail([none, loc[1]], axis=1) + product(st[1], y1)
        back = tail([jnp.where(late, 0.0, ar[1, :, :W].T), ar[2, :, W:]], axis=1)
        x2 = product(inv[0, 1], y2 + back + product(ar[2, :, :W], y2), 0)
        out[0] = product(inv[0, 0], y1 - product(cou[0, 1], x2, 0), 0)
        out[1] = x2

    return call(kernel, [shaped(2, W, 2 * W)], around, inverses, couplings, local, steps, flops=1e8)[0]


def arrive(got, swapped, mask, *waits):
    def kernel(g, sw, *refs):
        out = refs[-1]

        @pl.when(bit(1))
        def _():
            out[...] = g[...]

        @pl.when(jnp.logical_not(bit(1)))
        def _():
            out[...] = jnp.where(bit(mask), 0.0, product(g[...], sw[2 * W :]))

    return call(kernel, [shaped(W, W)], got, swapped, *waits)[0]


def finish(comes, sent, response, samples, lapx, lapy):
    def kernel(c, se, resp, s, lx, ly, white, grad):
        v = c[...] + se[...]
        r = resp[...].reshape(2 * W, 2 * W)
        w = (r[:, W:] + product(r[:, :W], v)).reshape(16, 16, W)
        white[...] = w
        grad[0] = jnp.sum(w * s[...], axis=2) * (1.0 / W)
        grad[1] = jnp.sum(w * lx[...], axis=2) * (1.0 / W)
        grad[2] = jnp.sum(w * ly[...], axis=2) * (1.0 / W)

    return call(kernel, [shaped(16, 16, W), shaped(3, 16, 16)], comes, sent, response, samples, lapx, lapy)


LEVELS = ((1, 1), (2, 2), (4, 6), (8, 8), (16, 24), (32, 32), (64, 64), (128, 192))
UP = 32


def body(samples, reaction, weight_x, weight_y, inverses, couplings):
    top = len(LEVELS) - 1
    evens = range(0, count(), 2)
    odds = range(1, count(), 2)
    x_one, x_two, y_one, y_two, samples, inverses, couplings = edges(samples, inverses, couplings)
    halo = []
    for axis, one, other in (("front", x_one, x_two), ("lat", y_one, y_two)):
        size = lax.axis_size(axis)
        pairs = [(i, (i + 1) % size) for i in range(1, size, 2)]
        halo.append(lax.ppermute(one, axis, [(i, i ^ 1) for i in range(size)]))
        halo.append(lax.ppermute(other, axis, pairs + [(j, i) for i, j in pairs]))
    steps, total = matrices(inverses, couplings, x_one)
    other_total = swap(total)
    chip = in_chip(total, other_total, *halo)
    got = arrived(send(chip, [(i, i ^ LEVELS[1][1]) for i in evens]))
    lapx, lapy, local, vectors = sources(
        samples, halo, reaction, weight_x, weight_y, inverses, steps, chip
    )
    other_vectors = swap(vectors)
    got, state, own = merge(
        got, LEVELS[1][0], LEVELS[0][0], chip, vectors, total, other_total, got_odd=other_vectors
    )
    swapped = swap(got)
    around = start_sides(other_total, other_vectors)
    waits = ()
    for at in range(1, top):
        pairs = [(i, i ^ LEVELS[at][1]) for i in odds]
        pairs += [(i, i ^ LEVELS[at + 1][1]) for i in evens if at + 1 < top]
        theirs, theirs_swapped, before = (got, swapped, state)
        got = send(before, pairs)
        last = LEVELS[top][0] if at + 1 == top else None
        got, state, own = merge(
            got, LEVELS[at + 1][0], LEVELS[at][0], before, before, own, theirs_swapped, last=last, waits=waits
        )
        swapped = swap(got if last is None else own)
        waits = (around,)
        around = widen(around, theirs, theirs_swapped, got, swapped, LEVELS[at][0])
    pairs = [(i, i ^ LEVELS[top][1]) for i in range(count()) if i & 1 or i & LEVELS[top][0]]
    got = send(state, pairs)
    response = respond(around, inverses, couplings, local, steps, LEVELS[top][0])
    comes = arrive(got, swapped, LEVELS[top][0], response)
    return tuple(finish(comes, swap(comes), response, samples, lapx, lapy))


def solution(mesh):
    placed = (
        P("front", "lat", None),
        P("front", "lat"),
        P("front", "lat"),
        P("front", "lat"),
        P("front", "lat", None, None),
        P("front", "lat", None, None),
    )
    return jax.shard_map(
        body,
        mesh=mesh,
        in_specs=placed,
        out_specs=(P("front", "lat", None), P(None, "front", "lat")),
        check_vma=False,
    )
```

```python
import jax
import jax.numpy as jnp
from jax import lax
from jax.experimental import pallas as pl
from jax.experimental.pallas import tpu as pltpu
from jax.sharding import PartitionSpec as P

F32 = jnp.float32
BF16 = jnp.bfloat16
W = 128


EVERY = ("front", "lat")


def count():
    return lax.axis_size("front") * lax.axis_size("lat")


def send(array, pairs):
    return lax.ppermute(array, EVERY, pairs)


def swap(array):
    return send(array, [(i, i ^ 1) for i in range(count())])


def call(kernel, outs, *operands, flops=4e7, same=None):
    vmem = pl.BlockSpec(memory_space=pltpu.VMEM)
    traffic = sum(a.size * 4 for a in operands) + sum(a.size * 4 for a in outs)
    return pl.pallas_call(
        kernel,
        out_shape=outs,
        in_specs=[vmem] * len(operands),
        out_specs=[vmem] * len(outs),
        input_output_aliases=same or {},
        compiler_params=pltpu.CompilerParams(vmem_limit_bytes=16 << 20),
        cost_estimate=pl.CostEstimate(flops=int(flops), bytes_accessed=int(traffic), transcendentals=0),
    )(*operands)


def shaped(*dims):
    return jax.ShapeDtypeStruct(dims, F32)


def two(value):
    high = value.astype(BF16)
    return high, (value - high.astype(F32)).astype(BF16)


def three(value):
    high = value.astype(BF16)
    rest = value - high.astype(F32)
    middle = rest.astype(BF16)
    return high, middle, (rest - middle.astype(F32)).astype(BF16)


def product(left, right, contract=1):
    def one(a, b):
        return lax.dot_general(a, b, (((contract,), (0,)), ((), ())), preferred_element_type=F32)

    (ah, al), (bh, bl) = (two(left), two(right))
    return one(ah, bh) + (one(ah, bl) + one(al, bh))


def exact(left, right, contract=1):
    def one(a, b):
        return lax.dot_general(a, b, (((contract,), (0,)), ((), ())), preferred_element_type=F32)

    (ah, am, al), (bh, bm, bl) = (three(left), three(right))
    return one(ah, bh) + ((one(ah, bm) + one(am, bh)) + (one(am, bm) + (one(ah, bl) + one(al, bh))))


def compose(first, second):
    (xa, za), (xb, zb) = (first, second)
    upper = product(jnp.concatenate([xb[:, :W], zb[:, :W]], axis=0), xa)
    tail = jnp.concatenate([xb[:, W:], zb[:, W:]], axis=0)
    upper = jnp.concatenate([upper[:, :W], upper[:, W:] + tail], axis=1)
    return (upper[:W], za + product(xa[:, :W], upper[W:], 0))


def compose_vectors(fa, maps, a, b):
    out = product(maps, a[:W]) + b
    return out[:W], a[W:] + product(fa, out[W:], 0)


def compose_matrices(a, b):
    out = product(b, a[:W])
    return out[:W], a[W:] + product(a[:W], out[W:], 0)


def forward(first, xb):
    out = product(xb[:, :W], first)
    return jnp.concatenate([out[:, :W], out[:, W:] + xb[:, W:]], axis=1)


def choose(flag, one, other):
    return tuple(jnp.where(flag, a, b) for a, b in zip(one, other))


def place():
    return lax.axis_index("front") * lax.axis_size("lat") + lax.axis_index("lat")


def bit(mask):
    return (place() & mask) != 0


def load(samples, inverses, couplings):
    def kernel(s, inv, cou, s_out, inv_out, cou_out, sems):
        pairs = ((s, s_out), (inv, inv_out), (cou, cou_out))
        copies = [pltpu.make_async_copy(a, b, sems.at[i]) for i, (a, b) in enumerate(pairs)]
        for copy in copies:
            copy.start()
        for copy in copies:
            copy.wait()

    outs = [shaped(*a.shape) for a in (samples, inverses, couplings)]
    return pl.pallas_call(
        kernel,
        out_shape=outs,
        in_specs=[pl.BlockSpec(memory_space=pltpu.HBM)] * 3,
        out_specs=[pl.BlockSpec(memory_space=pltpu.VMEM)] * len(outs),
        scratch_shapes=[pltpu.SemaphoreType.DMA((3,))],
        compiler_params=pltpu.CompilerParams(vmem_limit_bytes=107 << 19),
        cost_estimate=pl.CostEstimate(flops=1, bytes_accessed=800000, transcendentals=0),
    )(samples, inverses, couplings)


def pack(*fields):
    def kernel(re, wx, wy, out):
        out[0] = re[...]
        out[1] = wx[...]
        out[2] = wy[...]

    return call(kernel, [shaped(3, *fields[0].shape)], *fields, flops=1)[0]


def edges(samples, other):
    def kernel(odd, even, x_one, x_two, y_one, y_two):
        up = bit(UP)
        for at, tile in enumerate((even, odd)):
            x_one[at] = jnp.where(up, tile[0], tile[15])
            x_two[at] = jnp.where(up, tile[15], tile[0])
        right = bit(2)
        y_one[...] = jnp.where(right, even[:, 0:1], odd[:, 15:16])
        y_two[...] = jnp.where(right, odd[:, 15:16], even[:, 0:1])

    x, y = (shaped(2, 16, W), shaped(16, 1, W))
    return call(kernel, [x, x, y, y], samples, other, flops=1)


def matrices(inverses, couplings, *waits):
    def kernel(inv, cou, *refs):
        steps, total = refs[-2:]
        f1 = -exact(inv[0, 0], cou[0, 0])
        f2 = -exact(inv[0, 1], cou[0, 1])
        steps[0] = f1
        steps[1] = f2
        both = exact(f2, f1)
        total[:W] = both
        total[W:] = exact(f1, f1 + exact(f2, both, 0), 0)

    return call(kernel, [shaped(2, W, W), shaped(2 * W, W)], inverses, couplings, *waits, flops=3e7)


def sources(samples, samples_other, halo, fields, fields_other, inv, inv_other, steps, steps_other, total, total_other, wait):
    def kernel(so, se, x1, x2, y1, y2, *refs):
        fo, fe, io, ie, sto, ste, to, te, _, theirs, mine, chip = refs

        @pl.when(bit(1))
        def _():
            tail = jnp.concatenate
            first, last = (lax.axis_index("front") == 0, lax.axis_index("front") == lax.axis_size("front") - 1)
            left, right = (lax.axis_index("lat") == 1, lax.axis_index("lat") == lax.axis_size("lat") - 1)
            xm, xp = choose(bit(UP), (x1[...], x2[...]), (x2[...], x1[...]))
            xm, xp = (jnp.where(first, 0.0, xm), jnp.where(last, 0.0, xp))
            ym, yp = choose(bit(2), (y1[...], y2[...]), (y2[...], y1[...]))
            ym, yp = (jnp.where(left, 0.0, ym), jnp.where(right, 0.0, yp))
            even, odd = (se[...], so[...])
            sides_y = ((ym, odd[:, 0:1]), (even[:, 15:16], yp))
            sets = ((even, fe, ie, ste, theirs), (odd, fo, io, sto, mine))
            both = []
            for at, (v, fields, inv, st, out) in enumerate(sets):
                before, after = sides_y[at]
                lx = 2.0 * v - tail([xm[at : at + 1], v[:-1]], axis=0) - tail([v[1:], xp[at : at + 1]], axis=0)
                ly = 2.0 * v - tail([before, v[:, :-1]], axis=1) - tail([v[:, 1:], after], axis=1)
                out[: 2 * W] = lx.reshape(2 * W, W)
                out[2 * W : 4 * W] = ly.reshape(2 * W, W)
                r = fields[0][:, :, None] * v + fields[1][:, :, None] * lx + fields[2][:, :, None] * ly
                r = r.reshape(2, W, W)
                b1 = exact(inv[0, 0], r[0])
                b2 = exact(inv[0, 1], r[1])
                f = exact(st[1], b1) + b2
                h = exact(st[0], b1 + exact(st[1], f, 0), 0)
                out[4 * W : 5 * W] = b1
                out[5 * W : 6 * W] = b2
                both.append((f, h))
            for out, (f, h) in ((theirs, both[1]), (mine, both[0])):
                out[6 * W : 7 * W] = f
                out[7 * W :] = h
            chip[:W], chip[W:] = compose_vectors(te[:W], to[...], tail(both[0], axis=0), tail(both[1], axis=0))

    outs = [shaped(8 * W, W), shaped(8 * W, W), shaped(2 * W, W)]
    operands = (samples, samples_other, *halo, fields, fields_other)
    operands += (inv, inv_other, steps, steps_other, total, total_other, wait)
    return call(kernel, outs, *operands, flops=6e9)


def in_chip(total, partner, *waits):
    def kernel(t, p, *refs):
        chip = refs[-1]
        a, b = choose(bit(1), (p[...], t[...]), (t[...], p[...]))
        chip[:W], chip[W:] = compose_matrices(a, b)

    return call(kernel, [shaped(2 * W, W)], total, partner, *waits)[0]


def begin(got, mask, chip, vectors):
    def kernel(g, ev, od, _, state):
        @pl.when(bit(1))
        def _():
            state[...] = od[...]

        @pl.when(jnp.logical_not(bit(1)))
        def _():
            a, b = choose(bit(mask), (g[...], ev[...]), (ev[...], g[...]))
            state[:W], state[W:] = compose_matrices(a, b)

    return call(kernel, [shaped(2 * W, W)] * 2, got, chip, vectors, same={0: 0})


def merge(got, bit_even, bit_odd, even, odd, own, theirs, last=None, waits=()):
    def kernel(g, ev, od, ow, th, *refs):
        state, block = refs[-2:]

        @pl.when(bit(1))
        def _():
            late = bit(bit_odd)
            a, b = choose(late, (g[...], od[...]), (od[...], g[...]))
            maps_a, maps_b = choose(late, (th[...], ow[...]), (ow[...], th[...]))
            tail = jnp.concatenate
            first = (tail([maps_a[:W], a[:W]], axis=1), tail([maps_a[W:], a[W:]], axis=1))
            second = (tail([maps_b[:W], b[:W]], axis=1), tail([maps_b[W:], b[W:]], axis=1))
            x, z = compose(first, second)
            if last is None:
                block[:W] = x[:, :W]
                block[W:] = z[:, :W]
                state[:W] = x[:, W:]
                state[W:] = z[:, W:]
            else:
                block[: 2 * W] = g[...]
                block[2 * W :] = x[:, W:]
                state[...] = jnp.where(bit(last), z[:, W:], x[:, W:])

        @pl.when(jnp.logical_not(bit(1)))
        def _():
            if last is not None:
                state[...] = ev[W:]
            else:
                late = bit(bit_even)
                a, b = choose(late, (g[...], ev[...]), (ev[...], g[...]))
                state[:W], state[W:] = compose_matrices(a, b)

    outs = [shaped(2 * W, W)] * 3 if last is None else [shaped(2 * W, W), shaped(W, W), shaped(3 * W, W)]
    operands = (got, even, odd, own, theirs) + tuple(waits)
    return call(kernel, outs, *operands, same={0: 0})


def arrived(array):
    def kernel(a, out):
        pass

    return call(kernel, [shaped(*array.shape)], array, flops=1e10, same={0: 0})[0]


def start_sides(matrices, mine, sent):
    def kernel(m, mi, se, out):
        odd = bit(1)
        v = jnp.where(odd, mi[6 * W :], se[6 * W :])
        row = lax.broadcasted_iota(jnp.int32, (W, 2 * W), 0)
        col = lax.broadcasted_iota(jnp.int32, (W, 2 * W), 1)
        eye = jnp.where(row == col, 1.0, 0.0).astype(F32)
        x = jnp.concatenate([m[:W], v[:W]], axis=1)
        out[0] = jnp.where(odd, x, eye)
        out[1] = jnp.where(odd, eye, x)
        out[2] = jnp.where(odd, 0.0, jnp.concatenate([m[W:], v[W:]], axis=1))

    return call(kernel, [shaped(3, W, 2 * W)], matrices, mine, sent, flops=1)[0]


def widen(around, theirs, theirs_swapped, got, got_swapped, mask):
    def kernel(s, te, to, go, ge, out):
        odd = bit(1)
        late = bit(mask)
        m = jnp.where(odd, to[...], te[...])
        v = jnp.where(odd, go[...], ge[: 2 * W])

        @pl.when(late)
        def _():
            out[0] = forward(jnp.concatenate([m[:W], v[:W]], axis=1), s[0])
            out[1:] = s[1:]

        @pl.when(jnp.logical_not(late))
        def _():
            out[0] = s[0]
            later = (jnp.concatenate([m[:W], v[:W]], axis=1), jnp.concatenate([m[W:], v[W:]], axis=1))
            out[1], out[2] = compose((s[1], s[2]), later)

    operands = (around, theirs, theirs_swapped, got, got_swapped)
    return call(kernel, [shaped(3, W, 2 * W)], *operands)[0]


def respond(around, inverses, couplings, mine, sent, steps, mask):
    def kernel(ar, inv, cou, mi, se, st, out):
        late = bit(mask)
        loc = jnp.where(bit(1), mi[4 * W : 6 * W], se[4 * W : 6 * W])
        tail = jnp.concatenate
        none = jnp.zeros((W, W), F32)
        incoming = tail([jnp.where(late, ar[0, :, :W], 0.0), ar[0, :, W:]], axis=1)
        y1 = tail([none, loc[:W]], axis=1) + product(st[0], incoming)
        y2 = tail([none, loc[W:]], axis=1) + product(st[1], y1)
        back = tail([jnp.where(late, 0.0, ar[1, :, :W].T), ar[2, :, W:]], axis=1)
        x2 = product(inv[0, 1], y2 + back + product(ar[2, :, :W], y2), 0)
        out[0] = product(inv[0, 0], y1 - product(cou[0, 1], x2, 0), 0)
        out[1] = x2

    return call(kernel, [shaped(2, W, 2 * W)], around, inverses, couplings, mine, sent, steps, flops=1e8)[0]


def arrive(got, swapped, mask, *waits):
    def kernel(g, sw, *refs):
        out = refs[-1]

        @pl.when(bit(1))
        def _():
            out[...] = g[...]

        @pl.when(jnp.logical_not(bit(1)))
        def _():
            out[...] = jnp.where(bit(mask), 0.0, product(g[...], sw[2 * W :]))

    return call(kernel, [shaped(W, W)], got, swapped, *waits)[0]


def finish(comes, swapped, response, samples, mine, sent):
    def kernel(c, sw, resp, s, mi, se, white, grad):
        v = c[...] + sw[...]
        r = resp[...].reshape(2 * W, 2 * W)
        w = r[:, W:] + product(r[:, :W], v)
        white[...] = w.reshape(16, 16, W)
        lap = jnp.where(bit(1), mi[: 4 * W], se[: 4 * W])
        for at, factor in enumerate((s[...].reshape(2 * W, W), lap[: 2 * W], lap[2 * W :])):
            grad[at] = jnp.sum((w * factor).reshape(16, 16, W), axis=2) * (1.0 / W)

    outs = [shaped(16, 16, W), shaped(3, 16, 16)]
    return call(kernel, outs, comes, swapped, response, samples, mine, sent)


LEVELS = ((1, 1), (2, 2), (4, 6), (8, 8), (16, 24), (32, 32), (64, 64), (128, 192))
UP = 32
IDLE = 32


def body(samples, reaction, weight_x, weight_y, inverses, couplings):
    top = len(LEVELS) - 1
    evens = range(0, count(), 2)
    odds = range(1, count(), 2)
    samples, inverses, couplings = load(samples, inverses, couplings)
    fields = pack(reaction, weight_x, weight_y)
    samples_other = swap(samples)
    inverses_other = swap(inverses)
    fields_other = swap(fields)
    steps, total = matrices(inverses, couplings)
    other_total = swap(total)
    steps_other = swap(steps)
    x_one, x_two, y_one, y_two = edges(samples, other=samples_other)
    chips = count() // 2
    width = lax.axis_size("lat") // 2
    step = [(i, i - i % width + (i + 1) % width) for i in range(1, chips, 2)]
    step += [(j, i) for i, j in step]
    climb = [(i, (i + UP) % count()) for i in range(count()) if i & UP]
    climb += [(j, i) for i, j in climb]
    halo = [
        send(x_one, [(i, i ^ UP) for i in range(count())]),
        send(x_two, climb),
        send(y_one, [(i, i ^ 2) for i in range(count())]),
        send(y_two, [(2 * i + core, 2 * j + core) for i, j in step for core in range(2)]),
    ]
    chip = in_chip(total, other_total, x_one)
    got = arrived(send(chip, [(i, i ^ LEVELS[1][1]) for i in evens] + [(i, i ^ IDLE) for i in odds]))
    parcel, mine, vectors = sources(
        samples,
        samples_other,
        halo,
        fields,
        fields_other,
        inverses,
        inverses_other,
        steps,
        steps_other,
        total,
        other_total,
        chip,
    )
    got, state = begin(got, LEVELS[1][0], chip, vectors)
    own = chip
    swapped = swap(got)
    sent = swap(parcel)
    around = start_sides(other_total, mine, sent)
    waits = ()
    for at in range(1, top):
        pairs = [(i, i ^ LEVELS[at][1]) for i in odds]
        pairs += [(i, i ^ LEVELS[at + 1][1]) for i in evens if at + 1 < top]
        theirs, theirs_swapped, before = (got, swapped, state)
        got = send(before, pairs)
        last = LEVELS[top][0] if at + 1 == top else None
        got, state, own = merge(
            got, LEVELS[at + 1][0], LEVELS[at][0], before, before, own, theirs_swapped, last, waits
        )
        swapped = swap(got if last is None else own)
        waits = (around,)
        around = widen(around, theirs, theirs_swapped, got, swapped, LEVELS[at][0])
    pairs = [(i, i ^ LEVELS[top][1]) for i in range(count())]
    got = send(state, pairs)
    response = respond(around, inverses, couplings, mine, sent, steps, LEVELS[top][0])
    comes = arrive(got, swapped, LEVELS[top][0], response)
    return tuple(finish(comes, swap(comes), response, samples, mine, sent))


def solution(mesh):
    placed = (
        P("front", "lat", None),
        P("front", "lat"),
        P("front", "lat"),
        P("front", "lat"),
        P("front", "lat", None, None),
        P("front", "lat", None, None),
    )
    return jax.shard_map(
        body,
        mesh=mesh,
        in_specs=placed,
        out_specs=(P("front", "lat", None), P(None, "front", "lat")),
        check_vma=False,
    )
```

```python
import jax
import jax.numpy as jnp
from jax import lax
from jax.experimental import pallas as pl
from jax.experimental.pallas import tpu as pltpu
from jax.sharding import PartitionSpec as P

F32 = jnp.float32
BF16 = jnp.bfloat16
W = 128


EVERY = ("front", "lat")


def count():
    return lax.axis_size("front") * lax.axis_size("lat")


def send(array, pairs):
    return lax.ppermute(array, EVERY, pairs)


def swap(array):
    return send(array, [(i, i ^ 1) for i in range(count())])


def call(kernel, outs, *operands, flops=4e7, same=None):
    vmem = pl.BlockSpec(memory_space=pltpu.VMEM)
    traffic = sum(a.size * 4 for a in operands) + sum(a.size * 4 for a in outs)
    return pl.pallas_call(
        kernel,
        out_shape=outs,
        in_specs=[vmem] * len(operands),
        out_specs=[vmem] * len(outs),
        input_output_aliases=same or {},
        compiler_params=pltpu.CompilerParams(vmem_limit_bytes=16 << 20),
        cost_estimate=pl.CostEstimate(flops=int(flops), bytes_accessed=int(traffic), transcendentals=0),
    )(*operands)


def shaped(*dims):
    return jax.ShapeDtypeStruct(dims, F32)


def two(value):
    high = value.astype(BF16)
    return high, (value - high.astype(F32)).astype(BF16)


def three(value):
    high = value.astype(BF16)
    rest = value - high.astype(F32)
    middle = rest.astype(BF16)
    return high, middle, (rest - middle.astype(F32)).astype(BF16)


def product(left, right, contract=1):
    def one(a, b):
        return lax.dot_general(a, b, (((contract,), (0,)), ((), ())), preferred_element_type=F32)

    (ah, al), (bh, bl) = (two(left), two(right))
    return one(ah, bh) + (one(ah, bl) + one(al, bh))


def exact(left, right, contract=1):
    def one(a, b):
        return lax.dot_general(a, b, (((contract,), (0,)), ((), ())), preferred_element_type=F32)

    (ah, am, al), (bh, bm, bl) = (three(left), three(right))
    return one(ah, bh) + ((one(ah, bm) + one(am, bh)) + (one(am, bm) + (one(ah, bl) + one(al, bh))))


def compose(first, second):
    (xa, za), (xb, zb) = (first, second)
    upper = product(jnp.concatenate([xb[:, :W], zb[:, :W]], axis=0), xa)
    tail = jnp.concatenate([xb[:, W:], zb[:, W:]], axis=0)
    upper = jnp.concatenate([upper[:, :W], upper[:, W:] + tail], axis=1)
    return (upper[:W], za + product(xa[:, :W], upper[W:], 0))


def compose_vectors(fa, maps, a, b):
    out = product(maps, a[:W]) + b
    return out[:W], a[W:] + product(fa, out[W:], 0)


def compose_matrices(a, b):
    out = product(b, a[:W])
    return out[:W], a[W:] + product(a[:W], out[W:], 0)


def forward(first, xb):
    out = product(xb[:, :W], first)
    return jnp.concatenate([out[:, :W], out[:, W:] + xb[:, W:]], axis=1)


def choose(flag, one, other):
    return tuple(jnp.where(flag, a, b) for a, b in zip(one, other))


def place():
    return lax.axis_index("front") * lax.axis_size("lat") + lax.axis_index("lat")


def bit(mask):
    return (place() & mask) != 0


def load(samples, inverses, couplings):
    def kernel(s, inv, cou, s_out, inv_out, cou_out, sems):
        pairs = ((s, s_out), (inv, inv_out), (cou, cou_out))
        copies = [pltpu.make_async_copy(a, b, sems.at[i]) for i, (a, b) in enumerate(pairs)]
        for copy in copies:
            copy.start()
        for copy in copies:
            copy.wait()

    outs = [shaped(*a.shape) for a in (samples, inverses, couplings)]
    return pl.pallas_call(
        kernel,
        out_shape=outs,
        in_specs=[pl.BlockSpec(memory_space=pltpu.HBM)] * 3,
        out_specs=[pl.BlockSpec(memory_space=pltpu.VMEM)] * len(outs),
        scratch_shapes=[pltpu.SemaphoreType.DMA((3,))],
        compiler_params=pltpu.CompilerParams(vmem_limit_bytes=107 << 19),
        cost_estimate=pl.CostEstimate(flops=1, bytes_accessed=800000, transcendentals=0),
    )(samples, inverses, couplings)


def pack(*fields):
    def kernel(re, wx, wy, out):
        out[0] = re[...]
        out[1] = wx[...]
        out[2] = wy[...]

    return call(kernel, [shaped(3, *fields[0].shape)], *fields, flops=1)[0]


def edges(samples, other):
    def kernel(odd, even, x_one, x_two, y_one, y_two):
        up = bit(UP)
        for at, tile in enumerate((even, odd)):
            x_one[at] = jnp.where(up, tile[0], tile[15])
            x_two[at] = jnp.where(up, tile[15], tile[0])
        right = bit(2)
        y_one[...] = jnp.where(right, even[:, 0:1], odd[:, 15:16])
        y_two[...] = jnp.where(right, odd[:, 15:16], even[:, 0:1])

    x, y = (shaped(2, 16, W), shaped(16, 1, W))
    return call(kernel, [x, x, y, y], samples, other, flops=1)


def matrices(inverses, couplings, *waits):
    def kernel(inv, cou, *refs):
        steps, total = refs[-2:]
        f1 = -exact(inv[0, 0], cou[0, 0])
        f2 = -exact(inv[0, 1], cou[0, 1])
        steps[0] = f1
        steps[1] = f2
        both = exact(f2, f1)
        total[:W] = both
        total[W:] = exact(f1, f1 + exact(f2, both, 0), 0)

    return call(kernel, [shaped(2, W, W), shaped(2 * W, W)], inverses, couplings, *waits, flops=3e7)


def sources(samples, samples_other, halo, fields, fields_other, inv, inv_other, steps, steps_other, total, total_other, wait):
    def kernel(so, se, x1, x2, y1, y2, *refs):
        fo, fe, io, ie, sto, ste, to, te, _, theirs, mine, chip = refs

        @pl.when(bit(1))
        def _():
            tail = jnp.concatenate
            first, last = (lax.axis_index("front") == 0, lax.axis_index("front") == lax.axis_size("front") - 1)
            left, right = (lax.axis_index("lat") == 1, lax.axis_index("lat") == lax.axis_size("lat") - 1)
            xm, xp = choose(bit(UP), (x1[...], x2[...]), (x2[...], x1[...]))
            xm, xp = (jnp.where(first, 0.0, xm), jnp.where(last, 0.0, xp))
            ym, yp = choose(bit(2), (y1[...], y2[...]), (y2[...], y1[...]))
            ym, yp = (jnp.where(left, 0.0, ym), jnp.where(right, 0.0, yp))
            even, odd = (se[...], so[...])
            sides_y = ((ym, odd[:, 0:1]), (even[:, 15:16], yp))
            sets = ((even, fe, ie, ste, theirs), (odd, fo, io, sto, mine))
            both = []
            for at, (v, fields, inv, st, out) in enumerate(sets):
                before, after = sides_y[at]
                lx = 2.0 * v - tail([xm[at : at + 1], v[:-1]], axis=0) - tail([v[1:], xp[at : at + 1]], axis=0)
                ly = 2.0 * v - tail([before, v[:, :-1]], axis=1) - tail([v[:, 1:], after], axis=1)
                out[: 2 * W] = lx.reshape(2 * W, W)
                out[2 * W : 4 * W] = ly.reshape(2 * W, W)
                r = fields[0][:, :, None] * v + fields[1][:, :, None] * lx + fields[2][:, :, None] * ly
                r = r.reshape(2, W, W)
                b1 = exact(inv[0, 0], r[0])
                b2 = exact(inv[0, 1], r[1])
                f = exact(st[1], b1) + b2
                h = exact(st[0], b1 + exact(st[1], f, 0), 0)
                out[4 * W : 5 * W] = b1
                out[5 * W : 6 * W] = b2
                both.append((f, h))
            for out, (f, h) in ((theirs, both[1]), (mine, both[0])):
                out[6 * W : 7 * W] = f
                out[7 * W :] = h
            chip[:W], chip[W:] = compose_vectors(te[:W], to[...], tail(both[0], axis=0), tail(both[1], axis=0))

    outs = [shaped(8 * W, W), shaped(8 * W, W), shaped(2 * W, W)]
    operands = (samples, samples_other, *halo, fields, fields_other)
    operands += (inv, inv_other, steps, steps_other, total, total_other, wait)
    return call(kernel, outs, *operands, flops=1.3e9)


def in_chip(total, partner, *waits):
    def kernel(t, p, *refs):
        chip = refs[-1]
        a, b = choose(bit(1), (p[...], t[...]), (t[...], p[...]))
        chip[:W], chip[W:] = compose_matrices(a, b)

    return call(kernel, [shaped(2 * W, W)], total, partner, *waits)[0]


def begin(got, mask, chip, vectors):
    def kernel(g, ev, od, _, state):
        @pl.when(bit(1))
        def _():
            state[...] = od[...]

        @pl.when(jnp.logical_not(bit(1)))
        def _():
            a, b = choose(bit(mask), (g[...], ev[...]), (ev[...], g[...]))
            state[:W], state[W:] = compose_matrices(a, b)

    return call(kernel, [shaped(2 * W, W)] * 2, got, chip, vectors, same={0: 0})


def merge(got, bit_even, bit_odd, even, odd, own, theirs, last=None, waits=()):
    def kernel(g, ev, od, ow, th, *refs):
        state, block = refs[-2:]

        @pl.when(bit(1))
        def _():
            late = bit(bit_odd)
            a, b = choose(late, (g[...], od[...]), (od[...], g[...]))
            maps_a, maps_b = choose(late, (th[...], ow[...]), (ow[...], th[...]))
            tail = jnp.concatenate
            first = (tail([maps_a[:W], a[:W]], axis=1), tail([maps_a[W:], a[W:]], axis=1))
            second = (tail([maps_b[:W], b[:W]], axis=1), tail([maps_b[W:], b[W:]], axis=1))
            x, z = compose(first, second)
            if last is None:
                block[:W] = x[:, :W]
                block[W:] = z[:, :W]
                state[:W] = x[:, W:]
                state[W:] = z[:, W:]
            else:
                block[: 2 * W] = g[...]
                block[2 * W :] = x[:, W:]
                state[...] = jnp.where(bit(last), z[:, W:], x[:, W:])

        @pl.when(jnp.logical_not(bit(1)))
        def _():
            if last is not None:
                state[...] = ev[W:]
            else:
                late = bit(bit_even)
                a, b = choose(late, (g[...], ev[...]), (ev[...], g[...]))
                state[:W], state[W:] = compose_matrices(a, b)

    outs = [shaped(2 * W, W)] * 3 if last is None else [shaped(2 * W, W), shaped(W, W), shaped(3 * W, W)]
    operands = (got, even, odd, own, theirs) + tuple(waits)
    return call(kernel, outs, *operands, same={0: 0})


def arrived(array):
    def kernel(a, out):
        pass

    return call(kernel, [shaped(*array.shape)], array, flops=1e10, same={0: 0})[0]


def start_sides(matrices, mine, sent):
    def kernel(m, mi, se, out):
        odd = bit(1)
        v = jnp.where(odd, mi[6 * W :], se[6 * W :])
        row = lax.broadcasted_iota(jnp.int32, (W, 2 * W), 0)
        col = lax.broadcasted_iota(jnp.int32, (W, 2 * W), 1)
        eye = jnp.where(row == col, 1.0, 0.0).astype(F32)
        x = jnp.concatenate([m[:W], v[:W]], axis=1)
        out[0] = jnp.where(odd, x, eye)
        out[1] = jnp.where(odd, eye, x)
        out[2] = jnp.where(odd, 0.0, jnp.concatenate([m[W:], v[W:]], axis=1))

    return call(kernel, [shaped(3, W, 2 * W)], matrices, mine, sent, flops=1)[0]


def widen(around, theirs, theirs_swapped, got, got_swapped, mask):
    def kernel(s, te, to, go, ge, out):
        odd = bit(1)
        late = bit(mask)
        m = jnp.where(odd, to[...], te[...])
        v = jnp.where(odd, go[...], ge[: 2 * W])

        @pl.when(late)
        def _():
            out[0] = forward(jnp.concatenate([m[:W], v[:W]], axis=1), s[0])
            out[1:] = s[1:]

        @pl.when(jnp.logical_not(late))
        def _():
            out[0] = s[0]
            later = (jnp.concatenate([m[:W], v[:W]], axis=1), jnp.concatenate([m[W:], v[W:]], axis=1))
            out[1], out[2] = compose((s[1], s[2]), later)

    operands = (around, theirs, theirs_swapped, got, got_swapped)
    return call(kernel, [shaped(3, W, 2 * W)], *operands)[0]


def respond(around, inverses, couplings, mine, sent, steps, mask):
    def kernel(ar, inv, cou, mi, se, st, out):
        late = bit(mask)
        loc = jnp.where(bit(1), mi[4 * W : 6 * W], se[4 * W : 6 * W])
        tail = jnp.concatenate
        none = jnp.zeros((W, W), F32)
        incoming = tail([jnp.where(late, ar[0, :, :W], 0.0), ar[0, :, W:]], axis=1)
        y1 = tail([none, loc[:W]], axis=1) + product(st[0], incoming)
        y2 = tail([none, loc[W:]], axis=1) + product(st[1], y1)
        back = tail([jnp.where(late, 0.0, ar[1, :, :W].T), ar[2, :, W:]], axis=1)
        x2 = product(inv[0, 1], y2 + back + product(ar[2, :, :W], y2), 0)
        out[0] = product(inv[0, 0], y1 - product(cou[0, 1], x2, 0), 0)
        out[1] = x2

    return call(kernel, [shaped(2, W, 2 * W)], around, inverses, couplings, mine, sent, steps, flops=1e8)[0]


def arrive(got, swapped, mask, *waits):
    def kernel(g, sw, *refs):
        out = refs[-1]

        @pl.when(bit(1))
        def _():
            out[...] = g[...]

        @pl.when(jnp.logical_not(bit(1)))
        def _():
            out[...] = jnp.where(bit(mask), 0.0, product(g[...], sw[2 * W :]))

    return call(kernel, [shaped(W, W)], got, swapped, *waits)[0]


def finish(comes, swapped, response, samples, mine, sent):
    def kernel(c, sw, resp, s, mi, se, white, grad):
        v = c[...] + sw[...]
        r = resp[...].reshape(2 * W, 2 * W)
        w = r[:, W:] + product(r[:, :W], v)
        white[...] = w.reshape(16, 16, W)
        lap = jnp.where(bit(1), mi[: 4 * W], se[: 4 * W])
        for at, factor in enumerate((s[...].reshape(2 * W, W), lap[: 2 * W], lap[2 * W :])):
            grad[at] = jnp.sum((w * factor).reshape(16, 16, W), axis=2) * (1.0 / W)

    outs = [shaped(16, 16, W), shaped(3, 16, 16)]
    return call(kernel, outs, comes, swapped, response, samples, mine, sent)


LEVELS = ((1, 1), (2, 2), (4, 6), (8, 8), (16, 24), (32, 32), (64, 64), (128, 192))
UP = 32
IDLE = 32


def body(samples, reaction, weight_x, weight_y, inverses, couplings):
    top = len(LEVELS) - 1
    evens = range(0, count(), 2)
    odds = range(1, count(), 2)
    samples, inverses, couplings = load(samples, inverses, couplings)
    fields = pack(reaction, weight_x, weight_y)
    samples_other = swap(samples)
    inverses_other = swap(inverses)
    fields_other = swap(fields)
    steps, total = matrices(inverses, couplings)
    other_total = swap(total)
    steps_other = swap(steps)
    x_one, x_two, y_one, y_two = edges(samples, other=samples_other)
    chips = count() // 2
    width = lax.axis_size("lat") // 2
    step = [(i, i - i % width + (i + 1) % width) for i in range(1, chips, 2)]
    step += [(j, i) for i, j in step]
    climb = [(i, (i + UP) % count()) for i in range(count()) if i & UP]
    climb += [(j, i) for i, j in climb]
    halo = [
        send(x_one, [(i, i ^ UP) for i in range(count())]),
        send(x_two, climb),
        send(y_one, [(i, i ^ 2) for i in range(count())]),
        send(y_two, [(2 * i + core, 2 * j + core) for i, j in step for core in range(2)]),
    ]
    chip = in_chip(total, other_total, x_one)
    got = arrived(send(chip, [(i, i ^ LEVELS[1][1]) for i in evens] + [(i, i ^ IDLE) for i in odds]))
    parcel, mine, vectors = sources(
        samples,
        samples_other,
        halo,
        fields,
        fields_other,
        inverses,
        inverses_other,
        steps,
        steps_other,
        total,
        other_total,
        chip,
    )
    got, state = begin(got, LEVELS[1][0], chip, vectors)
    own = chip
    swapped = swap(got)
    sent = swap(parcel)
    around = start_sides(other_total, mine, sent)
    waits = ()
    for at in range(1, top):
        pairs = [(i, i ^ LEVELS[at][1]) for i in odds]
        pairs += [(i, i ^ LEVELS[at + 1][1]) for i in evens if at + 1 < top]
        theirs, theirs_swapped, before = (got, swapped, state)
        got = send(before, pairs)
        last = LEVELS[top][0] if at + 1 == top else None
        got, state, own = merge(
            got, LEVELS[at + 1][0], LEVELS[at][0], before, before, own, theirs_swapped, last, waits
        )
        swapped = swap(got if last is None else own)
        waits = (around,)
        around = widen(around, theirs, theirs_swapped, got, swapped, LEVELS[at][0])
    pairs = [(i, i ^ LEVELS[top][1]) for i in range(count())]
    got = send(state, pairs)
    response = respond(around, inverses, couplings, mine, sent, steps, LEVELS[top][0])
    comes = arrive(got, swapped, LEVELS[top][0], response)
    return tuple(finish(comes, swap(comes), response, samples, mine, sent))


def solution(mesh):
    placed = (
        P("front", "lat", None),
        P("front", "lat"),
        P("front", "lat"),
        P("front", "lat"),
        P("front", "lat", None, None),
        P("front", "lat", None, None),
    )
    return jax.shard_map(
        body,
        mesh=mesh,
        in_specs=placed,
        out_specs=(P("front", "lat", None), P(None, "front", "lat")),
        check_vma=False,
    )
```

```python
import jax
import jax.numpy as jnp
from jax import lax
from jax.experimental import pallas as pl
from jax.experimental.pallas import tpu as pltpu
from jax.sharding import PartitionSpec as P

F32 = jnp.float32
BF16 = jnp.bfloat16
W = 128


EVERY = ("front", "lat")


def count():
    return lax.axis_size("front") * lax.axis_size("lat")


def send(array, pairs):
    return lax.ppermute(array, EVERY, pairs)


def swap(array):
    return send(array, [(i, i ^ 1) for i in range(count())])


def call(kernel, outs, *operands, flops=4e7, same=None):
    vmem = pl.BlockSpec(memory_space=pltpu.VMEM)
    traffic = sum(a.size * 4 for a in operands) + sum(a.size * 4 for a in outs)
    return pl.pallas_call(
        kernel,
        out_shape=outs,
        in_specs=[vmem] * len(operands),
        out_specs=[vmem] * len(outs),
        input_output_aliases=same or {},
        compiler_params=pltpu.CompilerParams(vmem_limit_bytes=16 << 20),
        cost_estimate=pl.CostEstimate(flops=int(flops), bytes_accessed=int(traffic), transcendentals=0),
    )(*operands)


def shaped(*dims):
    return jax.ShapeDtypeStruct(dims, F32)


def two(value):
    high = value.astype(BF16)
    return high, (value - high.astype(F32)).astype(BF16)


def three(value):
    high = value.astype(BF16)
    rest = value - high.astype(F32)
    middle = rest.astype(BF16)
    return high, middle, (rest - middle.astype(F32)).astype(BF16)


def product(left, right, contract=1):
    def one(a, b):
        return lax.dot_general(a, b, (((contract,), (0,)), ((), ())), preferred_element_type=F32)

    (ah, al), (bh, bl) = (two(left), two(right))
    return one(ah, bh) + (one(ah, bl) + one(al, bh))


def exact(left, right, contract=1):
    def one(a, b):
        return lax.dot_general(a, b, (((contract,), (0,)), ((), ())), preferred_element_type=F32)

    (ah, am, al), (bh, bm, bl) = (three(left), three(right))
    return one(ah, bh) + ((one(ah, bm) + one(am, bh)) + (one(am, bm) + (one(ah, bl) + one(al, bh))))


def compose(first, second):
    (xa, za), (xb, zb) = (first, second)
    upper = product(jnp.concatenate([xb[:, :W], zb[:, :W]], axis=0), xa)
    tail = jnp.concatenate([xb[:, W:], zb[:, W:]], axis=0)
    upper = jnp.concatenate([upper[:, :W], upper[:, W:] + tail], axis=1)
    return (upper[:W], za + product(xa[:, :W], upper[W:], 0))


def compose_vectors(fa, maps, a, b):
    out = product(maps, a[:W]) + b
    return out[:W], a[W:] + product(fa, out[W:], 0)


def compose_matrices(a, b):
    out = product(b, a[:W])
    return out[:W], a[W:] + product(a[:W], out[W:], 0)


def forward(first, xb):
    out = product(xb[:, :W], first)
    return jnp.concatenate([out[:, :W], out[:, W:] + xb[:, W:]], axis=1)


def choose(flag, one, other):
    return tuple(jnp.where(flag, a, b) for a, b in zip(one, other))


def place():
    return lax.axis_index("front") * lax.axis_size("lat") + lax.axis_index("lat")


def bit(mask):
    return (place() & mask) != 0


def load(samples, inverses, couplings):
    def kernel(s, inv, cou, s_out, inv_out, cou_out, sems):
        pairs = ((s, s_out), (inv, inv_out), (cou, cou_out))
        copies = [pltpu.make_async_copy(a, b, sems.at[i]) for i, (a, b) in enumerate(pairs)]
        for copy in copies:
            copy.start()
        for copy in copies:
            copy.wait()

    outs = [shaped(*a.shape) for a in (samples, inverses, couplings)]
    return pl.pallas_call(
        kernel,
        out_shape=outs,
        in_specs=[pl.BlockSpec(memory_space=pltpu.HBM)] * 3,
        out_specs=[pl.BlockSpec(memory_space=pltpu.VMEM)] * len(outs),
        scratch_shapes=[pltpu.SemaphoreType.DMA((3,))],
        compiler_params=pltpu.CompilerParams(vmem_limit_bytes=107 << 19),
        cost_estimate=pl.CostEstimate(flops=1, bytes_accessed=800000, transcendentals=0),
    )(samples, inverses, couplings)


def pack(*fields):
    def kernel(re, wx, wy, out):
        out[0] = re[...]
        out[1] = wx[...]
        out[2] = wy[...]

    return call(kernel, [shaped(3, *fields[0].shape)], *fields, flops=1)[0]


def edges(samples, other):
    def kernel(odd, even, x_one, x_two, y_one, y_two):
        up = bit(UP)
        for at, tile in enumerate((even, odd)):
            x_one[at] = jnp.where(up, tile[0], tile[15])
            x_two[at] = jnp.where(up, tile[15], tile[0])
        right = bit(2)
        y_one[...] = jnp.where(right, even[:, 0:1], odd[:, 15:16])
        y_two[...] = jnp.where(right, odd[:, 15:16], even[:, 0:1])

    x, y = (shaped(2, 16, W), shaped(16, 1, W))
    return call(kernel, [x, x, y, y], samples, other, flops=1)


def matrices(inverses, couplings, *waits):
    def kernel(inv, cou, *refs):
        steps, total = refs[-2:]
        f1 = -exact(inv[0, 0], cou[0, 0])
        f2 = -exact(inv[0, 1], cou[0, 1])
        steps[0] = f1
        steps[1] = f2
        both = exact(f2, f1)
        total[:W] = both
        total[W:] = exact(f1, f1 + exact(f2, both, 0), 0)

    return call(kernel, [shaped(2, W, W), shaped(2 * W, W)], inverses, couplings, *waits, flops=3e7)


def sources(samples, samples_other, halo, fields, fields_other, inv, inv_other, steps, steps_other, total, total_other, wait):
    def kernel(so, se, x1, x2, y1, y2, *refs):
        fo, fe, io, ie, sto, ste, to, te, _, theirs, mine, chip = refs

        @pl.when(bit(1))
        def _():
            tail = jnp.concatenate
            first, last = (lax.axis_index("front") == 0, lax.axis_index("front") == lax.axis_size("front") - 1)
            left, right = (lax.axis_index("lat") == 1, lax.axis_index("lat") == lax.axis_size("lat") - 1)
            xm, xp = choose(bit(UP), (x1[...], x2[...]), (x2[...], x1[...]))
            xm, xp = (jnp.where(first, 0.0, xm), jnp.where(last, 0.0, xp))
            ym, yp = choose(bit(2), (y1[...], y2[...]), (y2[...], y1[...]))
            ym, yp = (jnp.where(left, 0.0, ym), jnp.where(right, 0.0, yp))
            even, odd = (se[...], so[...])
            sides_y = ((ym, odd[:, 0:1]), (even[:, 15:16], yp))
            sets = ((even, fe, ie, ste, theirs), (odd, fo, io, sto, mine))
            both = []
            for at, (v, fields, inv, st, out) in enumerate(sets):
                before, after = sides_y[at]
                lx = 2.0 * v - tail([xm[at : at + 1], v[:-1]], axis=0) - tail([v[1:], xp[at : at + 1]], axis=0)
                ly = 2.0 * v - tail([before, v[:, :-1]], axis=1) - tail([v[:, 1:], after], axis=1)
                out[: 2 * W] = lx.reshape(2 * W, W)
                out[2 * W : 4 * W] = ly.reshape(2 * W, W)
                r = fields[0][:, :, None] * v + fields[1][:, :, None] * lx + fields[2][:, :, None] * ly
                r = r.reshape(2, W, W)
                b1 = exact(inv[0, 0], r[0])
                b2 = exact(inv[0, 1], r[1])
                f = exact(st[1], b1) + b2
                h = exact(st[0], b1 + exact(st[1], f, 0), 0)
                out[4 * W : 5 * W] = b1
                out[5 * W : 6 * W] = b2
                both.append((f, h))
            for out, (f, h) in ((theirs, both[1]), (mine, both[0])):
                out[6 * W : 7 * W] = f
                out[7 * W :] = h
            chip[:W], chip[W:] = compose_vectors(te[:W], to[...], tail(both[0], axis=0), tail(both[1], axis=0))

    outs = [shaped(8 * W, W), shaped(8 * W, W), shaped(2 * W, W)]
    operands = (samples, samples_other, *halo, fields, fields_other)
    operands += (inv, inv_other, steps, steps_other, total, total_other, wait)
    return call(kernel, outs, *operands, flops=1.3e9)


def in_chip(total, partner, *waits):
    def kernel(t, p, *refs):
        chip = refs[-1]
        a, b = choose(bit(1), (p[...], t[...]), (t[...], p[...]))
        chip[:W], chip[W:] = compose_matrices(a, b)

    return call(kernel, [shaped(2 * W, W)], total, partner, *waits)[0]


def begin(got, mask, chip, vectors):
    def kernel(g, ev, od, _, state):
        @pl.when(bit(1))
        def _():
            state[...] = od[...]

        @pl.when(jnp.logical_not(bit(1)))
        def _():
            a, b = choose(bit(mask), (g[...], ev[...]), (ev[...], g[...]))
            state[:W], state[W:] = compose_matrices(a, b)

    return call(kernel, [shaped(2 * W, W)] * 2, got, chip, vectors, same={0: 0})


def merge(got, bit_even, bit_odd, even, odd, own, theirs, last=None, waits=()):
    def kernel(g, ev, od, ow, th, *refs):
        state, block = refs[-2:]

        @pl.when(bit(1))
        def _():
            late = bit(bit_odd)
            a, b = choose(late, (g[...], od[...]), (od[...], g[...]))
            maps_a, maps_b = choose(late, (th[...], ow[...]), (ow[...], th[...]))
            tail = jnp.concatenate
            first = (tail([maps_a[:W], a[:W]], axis=1), tail([maps_a[W:], a[W:]], axis=1))
            second = (tail([maps_b[:W], b[:W]], axis=1), tail([maps_b[W:], b[W:]], axis=1))
            x, z = compose(first, second)
            if last is None:
                block[:W] = x[:, :W]
                block[W:] = z[:, :W]
                state[:W] = x[:, W:]
                state[W:] = z[:, W:]
            else:
                block[: 2 * W] = g[...]
                block[2 * W :] = x[:, W:]
                state[...] = jnp.where(bit(last), z[:, W:], x[:, W:])

        @pl.when(jnp.logical_not(bit(1)))
        def _():
            if last is not None:
                state[...] = ev[W:]
            else:
                late = bit(bit_even)
                a, b = choose(late, (g[...], ev[...]), (ev[...], g[...]))
                state[:W], state[W:] = compose_matrices(a, b)

    outs = [shaped(2 * W, W)] * 3 if last is None else [shaped(2 * W, W), shaped(W, W), shaped(3 * W, W)]
    operands = (got, even, odd, own, theirs) + tuple(waits)
    return call(kernel, outs, *operands, same={0: 0})


def arrived(array):
    def kernel(a, out):
        pass

    return call(kernel, [shaped(*array.shape)], array, flops=1e10, same={0: 0})[0]


def start_sides(matrices, mine, sent):
    def kernel(m, mi, se, out):
        odd = bit(1)
        v = jnp.where(odd, mi[6 * W :], se[6 * W :])
        row = lax.broadcasted_iota(jnp.int32, (W, 2 * W), 0)
        col = lax.broadcasted_iota(jnp.int32, (W, 2 * W), 1)
        eye = jnp.where(row == col, 1.0, 0.0).astype(F32)
        x = jnp.concatenate([m[:W], v[:W]], axis=1)
        out[0] = jnp.where(odd, x, eye)
        out[1] = jnp.where(odd, eye, x)
        out[2] = jnp.where(odd, 0.0, jnp.concatenate([m[W:], v[W:]], axis=1))

    return call(kernel, [shaped(3, W, 2 * W)], matrices, mine, sent, flops=1)[0]


def widen(around, theirs, theirs_swapped, got, got_swapped, mask):
    def kernel(s, te, to, go, ge, out):
        odd = bit(1)
        late = bit(mask)
        m = jnp.where(odd, to[...], te[...])
        v = jnp.where(odd, go[...], ge[: 2 * W])

        @pl.when(late)
        def _():
            out[0] = forward(jnp.concatenate([m[:W], v[:W]], axis=1), s[0])
            out[1:] = s[1:]

        @pl.when(jnp.logical_not(late))
        def _():
            out[0] = s[0]
            later = (jnp.concatenate([m[:W], v[:W]], axis=1), jnp.concatenate([m[W:], v[W:]], axis=1))
            out[1], out[2] = compose((s[1], s[2]), later)

    operands = (around, theirs, theirs_swapped, got, got_swapped)
    return call(kernel, [shaped(3, W, 2 * W)], *operands)[0]


def respond(around, inverses, couplings, mine, sent, steps, mask):
    def kernel(ar, inv, cou, mi, se, st, out):
        late = bit(mask)
        loc = jnp.where(bit(1), mi[4 * W : 6 * W], se[4 * W : 6 * W])
        tail = jnp.concatenate
        none = jnp.zeros((W, W), F32)
        incoming = tail([jnp.where(late, ar[0, :, :W], 0.0), ar[0, :, W:]], axis=1)
        y1 = tail([none, loc[:W]], axis=1) + product(st[0], incoming)
        y2 = tail([none, loc[W:]], axis=1) + product(st[1], y1)
        back = tail([jnp.where(late, 0.0, ar[1, :, :W].T), ar[2, :, W:]], axis=1)
        x2 = product(inv[0, 1], y2 + back + product(ar[2, :, :W], y2), 0)
        out[0] = product(inv[0, 0], y1 - product(cou[0, 1], x2, 0), 0)
        out[1] = x2

    return call(kernel, [shaped(2, W, 2 * W)], around, inverses, couplings, mine, sent, steps, flops=1e8)[0]


def arrive(got, swapped, mask, *waits):
    def kernel(g, sw, *refs):
        out = refs[-1]

        @pl.when(bit(1))
        def _():
            out[...] = g[...]

        @pl.when(jnp.logical_not(bit(1)))
        def _():
            out[...] = jnp.where(bit(mask), 0.0, product(g[...], sw[2 * W :]))

    return call(kernel, [shaped(W, W)], got, swapped, *waits)[0]


def finish(comes, swapped, response, samples, mine, sent):
    def kernel(c, sw, resp, s, mi, se, white, grad, held, sem):
        v = c[...] + sw[...]
        r = resp[...].reshape(2 * W, 2 * W)
        w = r[:, W:] + product(r[:, :W], v)
        held[...] = w.reshape(16, 16, W)
        copy = pltpu.make_async_copy(held, white, sem)
        copy.start()
        lap = jnp.where(bit(1), mi[: 4 * W], se[: 4 * W])
        for at, factor in enumerate((s[...].reshape(2 * W, W), lap[: 2 * W], lap[2 * W :])):
            grad[at] = jnp.sum((w * factor).reshape(16, 16, W), axis=2) * (1.0 / W)
        copy.wait()

    vmem = pl.BlockSpec(memory_space=pltpu.VMEM)
    return pl.pallas_call(
        kernel,
        out_shape=[shaped(16, 16, W), shaped(3, 16, 16)],
        in_specs=[vmem] * 6,
        out_specs=[pl.BlockSpec(memory_space=pltpu.HBM), vmem],
        scratch_shapes=[pltpu.VMEM((16, 16, W), F32), pltpu.SemaphoreType.DMA],
        compiler_params=pltpu.CompilerParams(vmem_limit_bytes=16 << 20),
        cost_estimate=pl.CostEstimate(flops=40000000, bytes_accessed=1400000, transcendentals=0),
    )(comes, swapped, response, samples, mine, sent)


LEVELS = ((1, 1), (2, 2), (4, 6), (8, 8), (16, 24), (32, 32), (64, 64), (128, 192))
UP = 32
IDLE = 32


def body(samples, reaction, weight_x, weight_y, inverses, couplings):
    top = len(LEVELS) - 1
    evens = range(0, count(), 2)
    odds = range(1, count(), 2)
    samples, inverses, couplings = load(samples, inverses, couplings)
    fields = pack(reaction, weight_x, weight_y)
    samples_other = swap(samples)
    inverses_other = swap(inverses)
    fields_other = swap(fields)
    steps, total = matrices(inverses, couplings)
    other_total = swap(total)
    steps_other = swap(steps)
    x_one, x_two, y_one, y_two = edges(samples, other=samples_other)
    chips = count() // 2
    width = lax.axis_size("lat") // 2
    step = [(i, i - i % width + (i + 1) % width) for i in range(1, chips, 2)]
    step += [(j, i) for i, j in step]
    climb = [(i, (i + UP) % count()) for i in range(count()) if i & UP]
    climb += [(j, i) for i, j in climb]
    halo = [
        send(x_one, [(i, i ^ UP) for i in range(count())]),
        send(x_two, climb),
        send(y_one, [(i, i ^ 2) for i in range(count())]),
        send(y_two, [(2 * i + core, 2 * j + core) for i, j in step for core in range(2)]),
    ]
    chip = in_chip(total, other_total, x_one)
    got = arrived(send(chip, [(i, i ^ LEVELS[1][1]) for i in evens] + [(i, i ^ IDLE) for i in odds]))
    parcel, mine, vectors = sources(
        samples,
        samples_other,
        halo,
        fields,
        fields_other,
        inverses,
        inverses_other,
        steps,
        steps_other,
        total,
        other_total,
        chip,
    )
    got, state = begin(got, LEVELS[1][0], chip, vectors)
    own = chip
    swapped = swap(got)
    sent = swap(parcel)
    around = start_sides(other_total, mine, sent)
    waits = ()
    for at in range(1, top):
        pairs = [(i, i ^ LEVELS[at][1]) for i in odds]
        pairs += [(i, i ^ LEVELS[at + 1][1]) for i in evens if at + 1 < top]
        theirs, theirs_swapped, before = (got, swapped, state)
        got = send(before, pairs)
        last = LEVELS[top][0] if at + 1 == top else None
        got, state, own = merge(
            got, LEVELS[at + 1][0], LEVELS[at][0], before, before, own, theirs_swapped, last, waits
        )
        swapped = swap(got if last is None else own)
        waits = (around,)
        around = widen(around, theirs, theirs_swapped, got, swapped, LEVELS[at][0])
    pairs = [(i, i ^ LEVELS[top][1]) for i in range(count())]
    got = send(state, pairs)
    response = respond(around, inverses, couplings, mine, sent, steps, LEVELS[top][0])
    comes = arrive(got, swapped, LEVELS[top][0], response)
    return tuple(finish(comes, swap(comes), response, samples, mine, sent))


def solution(mesh):
    placed = (
        P("front", "lat", None),
        P("front", "lat"),
        P("front", "lat"),
        P("front", "lat"),
        P("front", "lat", None, None),
        P("front", "lat", None, None),
    )
    return jax.shard_map(
        body,
        mesh=mesh,
        in_specs=placed,
        out_specs=(P("front", "lat", None), P(None, "front", "lat")),
        check_vma=False,
    )
```
